32 devices in a mesh: job: 2 (over x), actor: 8 (over z, y), tp: 2 (over core).
Axes of the slice: x: 2, y: 2, z: 4, core: 2. Of those that a mesh axis runs over, the one named last changes fastest.
Arguments:
- leaf_states: bfloat16 [4096, 5120], P(('job', 'actor')), parts along dimension 0, may hold values from -6 to 6
- norm_gain: bfloat16 [5120], replicated, may hold values from 0.25 to 1.75
- wq_quant: bfloat16 [5120, 2560], P('actor', 'tp'), may hold values from -4 to 4
- wq_scale: float32 [40, 20], P(None, 'tp'), may hold values from 0.0069877123 to 0.02795085
- key_weight_quantized: bfloat16 [5120, 512], P('actor', 'tp'), may hold values from -4 to 4
- key_weight_scale: float32 [40, 4], P(None, 'tp'), may hold values from 0.0069877123 to 0.02795085
- value_weight_quantized: bfloat16 [5120, 512], P('actor', 'tp'), may hold values from -4 to 4
- value_weight_scale: float32 [40, 4], P(None, 'tp'), may hold values from 0.0069877123 to 0.02795085
- wo_quant: bfloat16 [2560, 5120], P('tp', 'actor'), may hold values from -4 to 4
- wo_scale: float32 [20, 40], P('tp'), may hold values from 0.019764235 to 0.07905694
- q_bias: bfloat16 [2560], P('tp'), may hold values from -2 to 2
- key_bias: bfloat16 [512], P('tp'), may hold values from -2 to 2
- value_bias: bfloat16 [512], P('tp'), may hold values from -3 to 3
- prefix_key_cache: bfloat16 [32, 2048, 512], P(('job', 'actor'), None, 'tp'), parts along dimension 0, may hold values from -140 to 140
- prefix_value_cache: bfloat16 [32, 2048, 512], P(('job', 'actor'), None, 'tp'), parts along dimension 0, may hold values from -15 to 15
- parent_prefix_slot: int32 [4096], P(('job', 'actor')), parts along dimension 0, may hold values from 0 to 1
- prefix_length: int32 [4096], P(('job', 'actor')), parts along dimension 0, may hold values from 1 to 2048, as said below
Outputs:
- attn_out: bfloat16 [4096, 5120], P(('job', 'actor')), parts along dimension 0
The draws below stay inside these ranges and needn't reach their ends.
There are 2 independent parts, one for each index of `job`. The reference program is written for one: setup_inputs(seed, part) draws one part's arguments, and reference() takes and returns one part's arrays. A program takes and returns all parts, laid end to end along the dimension named above; an argument that names none is the same for every part. Nothing has to cross between parts.
Inputs may be any that keep to these rules, and one draw needn't show every extreme that they name: parent_prefix_slot numbers the leaf's prefix among the 2 prefixes of its own actor replica's block of the cache (leaf t belongs to replica t // 256, whose prefixes are cache rows 2 r to 2 r + 1). `prefix_length`: the first leaf of every actor replica sees all 2048 cached positions.
All inputs are finite; a program needn't handle non-finite values.
Results may differ from the reference program's by a relative error of at most 0.0045.
The reference program's roundings to bfloat16 on the way (of `normed` and `attended`) count: a program that leaves them out, or rounds other values in their place, can miss the bound.
Values may be sent and summed in bfloat16 or wider, within the bound.
A program may use at most 192 MiB of HBM per device.

```python
import math
import jax
import jax.numpy as jnp
from jax import lax

MODEL_WIDTH = 5120
HEAD_WIDTH = 128
QUERY_HEADS = 20
KEY_VALUE_HEADS = 4
SCALE_BLOCK = 128
CONTEXT_LENGTH = 2048
PREFIX_PER_ACTOR = 2
LEAF_PER_ACTOR = 256
LEAF_TOTAL = 2048
PREFIX_TOTAL = 16
N_ACTOR = 8


def draw_prefix_key_cache(key, part):
    first = jax.random.fold_in(jax.random.fold_in(key, 11), 0)
    array_shape = (PREFIX_TOTAL, CONTEXT_LENGTH, KEY_VALUE_HEADS * HEAD_WIDTH)
    base = jnp.clip(2.0 * jax.random.normal(first, array_shape, jnp.float32), -12.0, 12.0)
    return base.astype(jnp.bfloat16)


def draw_prefix_length(key, part):
    drawn = jax.random.randint(jax.random.fold_in(key, 23), (LEAF_TOTAL,), 1, CONTEXT_LENGTH + 1, dtype=jnp.int32)
    return drawn.at[::LEAF_PER_ACTOR].set(CONTEXT_LENGTH)


def shared_signs(key):
    flipped = jax.random.bernoulli(jax.random.fold_in(key, 31), 0.5, (KEY_VALUE_HEADS, HEAD_WIDTH))
    return jnp.where(flipped, 1.0, -1.0).astype(jnp.float32)


def draw_q_bias(key, part):
    sign_table = shared_signs(key)
    magnitude = jax.random.uniform(jax.random.fold_in(key, 37), (QUERY_HEADS, HEAD_WIDTH), jnp.float32, 0.5, 1.5)
    spread_signs = jnp.repeat(sign_table, QUERY_HEADS // KEY_VALUE_HEADS, axis=0)
    return (spread_signs * magnitude).reshape(QUERY_HEADS * HEAD_WIDTH).astype(jnp.bfloat16)


def draw_key_bias(key, part):
    sign_table = shared_signs(key)
    magnitude = jax.random.uniform(jax.random.fold_in(key, 41), (KEY_VALUE_HEADS, HEAD_WIDTH), jnp.float32, 0.5, 1.5)
    return (sign_table * magnitude).reshape(KEY_VALUE_HEADS * HEAD_WIDTH).astype(jnp.bfloat16)


def touch_ends(result, own_key, smallest, top_value):
    dims = result.shape
    index_at = [jax.random.randint(jax.random.fold_in(own_key, axis), (), 0, dims[axis]) for axis in range(len(dims))]
    result = result.at[tuple(index_at)].set(smallest)
    longest = dims.index(max(dims))
    index_at[longest] = (index_at[longest] + 1) % dims[longest]
    return result.at[tuple(index_at)].set(top_value)


def block_scale(rng, dims, cuts, least, largest):
    gain = 1.0
    for axis_at, shards_of in cuts:
        draws = jax.random.uniform(jax.random.fold_in(jax.random.fold_in(rng, 6), axis_at), (shards_of,), jnp.float32, least / len(cuts), largest / len(cuts))
        gain = gain * jnp.repeat(jnp.exp(draws), dims[axis_at] // shards_of).reshape((-1,) + (1,) * (len(dims) - 1 - axis_at))
    return gain


def noise(key, dims, scale, reach, cuts=(), kind=jnp.bfloat16):
    factor_of = block_scale(key, dims, cuts, -0.22, 0.18) if cuts else 1.0
    values = jax.random.normal(key, dims, jnp.float32) * scale * factor_of
    return jnp.minimum(jnp.maximum(values, -reach), reach).astype(kind)


def setup_inputs(seed: int = 0, part: int = 0) -> dict:
    key_list = jax.random.split(jax.random.key(seed), 18)
    part_splits = jax.random.split(jax.random.fold_in(key_list[17], part), 18)
    leaf_states = noise(part_splits[0], (LEAF_TOTAL, MODEL_WIDTH), 1.0, 6.0, ((0, 8),))
    norm_gain = jnp.clip(1.0 + 0.15 * jax.random.normal(key_list[1], (MODEL_WIDTH,), jnp.float32), 0.25, 1.75).astype(jnp.bfloat16)
    wq_quant = noise(key_list[2], (MODEL_WIDTH, QUERY_HEADS * HEAD_WIDTH), 1.0, 4.0, ((0, 8), (1, 2)))
    wq_scale = jnp.clip(jnp.exp(math.log(0.02795085) - 1.3862944 * jax.random.uniform(key_list[3], (MODEL_WIDTH // SCALE_BLOCK, QUERY_HEADS * HEAD_WIDTH // SCALE_BLOCK), jnp.float32) ** block_scale(key_list[3], (MODEL_WIDTH // SCALE_BLOCK, QUERY_HEADS * HEAD_WIDTH // SCALE_BLOCK), ((1, 2),), -0.2, 0.2)), 0.0069877123, 0.02795085)
    key_weight_quantized = noise(key_list[4], (MODEL_WIDTH, KEY_VALUE_HEADS * HEAD_WIDTH), 1.0, 4.0, ((0, 8), (1, 2)))
    key_weight_scale = jnp.clip(jnp.exp(math.log(0.02795085) - 1.3862944 * jax.random.uniform(key_list[5], (MODEL_WIDTH // SCALE_BLOCK, KEY_VALUE_HEADS * HEAD_WIDTH // SCALE_BLOCK), jnp.float32) ** block_scale(key_list[5], (MODEL_WIDTH // SCALE_BLOCK, KEY_VALUE_HEADS * HEAD_WIDTH // SCALE_BLOCK), ((1, 2),), -0.2, 0.2)), 0.0069877123, 0.02795085)
    value_weight_quantized = noise(key_list[6], (MODEL_WIDTH, KEY_VALUE_HEADS * HEAD_WIDTH), 1.0, 4.0, ((0, 8), (1, 2)))
    value_weight_scale = jnp.clip(jnp.exp(math.log(0.02795085) - 1.3862944 * jax.random.uniform(key_list[7], (MODEL_WIDTH // SCALE_BLOCK, KEY_VALUE_HEADS * HEAD_WIDTH // SCALE_BLOCK), jnp.float32) ** block_scale(key_list[7], (MODEL_WIDTH // SCALE_BLOCK, KEY_VALUE_HEADS * HEAD_WIDTH // SCALE_BLOCK), ((1, 2),), -0.2, 0.2)), 0.0069877123, 0.02795085)
    wo_quant = noise(key_list[8], (QUERY_HEADS * HEAD_WIDTH, MODEL_WIDTH), 1.0, 4.0, ((0, 2), (1, 8)))
    wo_scale = jnp.clip(jnp.exp(math.log(0.07905694) - 1.3862944 * jax.random.uniform(key_list[9], (QUERY_HEADS * HEAD_WIDTH // SCALE_BLOCK, MODEL_WIDTH // SCALE_BLOCK), jnp.float32) ** block_scale(key_list[9], (QUERY_HEADS * HEAD_WIDTH // SCALE_BLOCK, MODEL_WIDTH // SCALE_BLOCK), ((0, 2),), -0.2, 0.2)), 0.019764235, 0.07905694)
    q_bias = draw_q_bias(jax.random.fold_in(key_list[17], 71), part)
    key_bias = draw_key_bias(jax.random.fold_in(key_list[17], 71), part)
    value_bias = noise(key_list[12], (KEY_VALUE_HEADS * HEAD_WIDTH,), 1.0, 3.0, ((0, 2),))
    prefix_key_cache = draw_prefix_key_cache(jax.random.fold_in(jax.random.fold_in(key_list[17], part), 71), part)
    prefix_value_cache = noise(part_splits[14], (PREFIX_TOTAL, CONTEXT_LENGTH, KEY_VALUE_HEADS * HEAD_WIDTH), 3.0, 15.0, ((0, 8), (2, 2)))
    parent_prefix_slot = touch_ends(jax.random.randint(part_splits[15], (LEAF_TOTAL,), 0, PREFIX_PER_ACTOR), jax.random.fold_in(part_splits[15], 1), 0, PREFIX_PER_ACTOR - 1).astype(jnp.int32)
    prefix_length = draw_prefix_length(jax.random.fold_in(jax.random.fold_in(key_list[17], part), 71), part)
    return {"leaf_states": leaf_states, "norm_gain": norm_gain, "wq_quant": wq_quant, "wq_scale": wq_scale, "key_weight_quantized": key_weight_quantized, "key_weight_scale": key_weight_scale, "value_weight_quantized": value_weight_quantized, "value_weight_scale": value_weight_scale, "wo_quant": wo_quant, "wo_scale": wo_scale, "q_bias": q_bias, "key_bias": key_bias, "value_bias": value_bias, "prefix_key_cache": prefix_key_cache, "prefix_value_cache": prefix_value_cache, "parent_prefix_slot": parent_prefix_slot, "prefix_length": prefix_length}


epsilon = 1e-06
rope_base = 1000000.0

def dequantize(quant, scale):
    expanded = jnp.repeat(jnp.repeat(scale, SCALE_BLOCK, axis=0), SCALE_BLOCK, axis=1)
    return (quant.astype(jnp.float32) * expanded).astype(jnp.bfloat16)

def apply_rotary(values, length):
    width = values.shape[-1]
    half_width = width // 2
    freqs = rope_base ** (-(jnp.arange(half_width, dtype=jnp.float32) * 2.0 / width))
    angles = length.astype(jnp.float32)[:, None] * freqs[None, :]
    cosine = jnp.cos(angles)[:, None, :]
    sine = jnp.sin(angles)[:, None, :]
    first = values[..., :half_width]
    second = values[..., half_width:]
    return jnp.concatenate([first * cosine - second * sine, second * cosine + first * sine], axis=-1)

def attend_single_head(query_vector, key_self, value_self, prefix_key_cache, prefix_value_cache, parent, length):
    scale_factor = 1.0 / math.sqrt(query_vector.shape[-1])
    query_wide = query_vector.astype(jnp.float32)
    self_score = lax.optimization_barrier(jnp.sum(query_wide * key_self.astype(jnp.float32)[:, None, :], axis=-1)) * scale_factor
    visible = (jnp.arange(prefix_key_cache.shape[1])[None, :] < length[:, None])[:, None, :]
    outcome = jnp.zeros(query_vector.shape, jnp.float32)
    for prefix_index in range(prefix_key_cache.shape[0]):
        scores = jnp.einsum('lge,ce->lgc', query_wide, prefix_key_cache[prefix_index].astype(jnp.float32)) * scale_factor
        highest = jnp.maximum(lax.optimization_barrier(jnp.max(jnp.where(visible, scores, -jnp.inf), axis=-1)), self_score)
        weights = jnp.where(visible, jnp.exp(scores - highest[..., None]), 0.0)
        self_weight = jnp.exp(self_score - highest)
        total = lax.optimization_barrier(jnp.sum(weights, axis=-1)) + self_weight
        rounded = lax.optimization_barrier(weights.astype(jnp.bfloat16)).astype(jnp.float32)
        self_rounded = lax.optimization_barrier(self_weight.astype(jnp.bfloat16)).astype(jnp.float32)
        mixed = jnp.einsum('lgc,ce->lge', rounded, prefix_value_cache[prefix_index].astype(jnp.float32))
        mixed = mixed + self_rounded[..., None] * value_self.astype(jnp.float32)[:, None, :]
        outcome = jnp.where((parent == prefix_index)[:, None, None], mixed / total[..., None], outcome)
    return outcome

def reference(leaf_states, norm_gain, wq_quant, wq_scale, key_weight_quantized, key_weight_scale, value_weight_quantized, value_weight_scale, wo_quant, wo_scale, q_bias, key_bias, value_bias, prefix_key_cache, prefix_value_cache, parent_prefix_slot, prefix_length):
    states = leaf_states.astype(jnp.float32)
    normed = (states * lax.rsqrt(lax.optimization_barrier(jnp.mean(states * states, axis=-1, keepdims=True)) + epsilon) * norm_gain.astype(jnp.float32)).astype(jnp.bfloat16)
    query_vector = jnp.dot(normed, dequantize(wq_quant, wq_scale), preferred_element_type=jnp.float32) + q_bias.astype(jnp.float32)
    fresh_key = jnp.dot(normed, dequantize(key_weight_quantized, key_weight_scale), preferred_element_type=jnp.float32) + key_bias.astype(jnp.float32)
    fresh_value = jnp.dot(normed, dequantize(value_weight_quantized, value_weight_scale), preferred_element_type=jnp.float32) + value_bias.astype(jnp.float32)
    query_vector = apply_rotary(query_vector.reshape(LEAF_TOTAL, QUERY_HEADS, HEAD_WIDTH), prefix_length).astype(jnp.bfloat16)
    fresh_key = apply_rotary(fresh_key.reshape(LEAF_TOTAL, KEY_VALUE_HEADS, HEAD_WIDTH), prefix_length).astype(jnp.bfloat16)
    fresh_value = fresh_value.reshape(LEAF_TOTAL, KEY_VALUE_HEADS, HEAD_WIDTH).astype(jnp.bfloat16)
    query_group = QUERY_HEADS // KEY_VALUE_HEADS
    block_grid = (query_vector.reshape(N_ACTOR, LEAF_PER_ACTOR, KEY_VALUE_HEADS, query_group, HEAD_WIDTH), fresh_key.reshape(N_ACTOR, LEAF_PER_ACTOR, KEY_VALUE_HEADS, HEAD_WIDTH), fresh_value.reshape(N_ACTOR, LEAF_PER_ACTOR, KEY_VALUE_HEADS, HEAD_WIDTH), prefix_key_cache.reshape(N_ACTOR, PREFIX_PER_ACTOR, CONTEXT_LENGTH, KEY_VALUE_HEADS, HEAD_WIDTH), prefix_value_cache.reshape(N_ACTOR, PREFIX_PER_ACTOR, CONTEXT_LENGTH, KEY_VALUE_HEADS, HEAD_WIDTH), parent_prefix_slot.reshape(N_ACTOR, LEAF_PER_ACTOR), prefix_length.reshape(N_ACTOR, LEAF_PER_ACTOR))

    def one_block(pieces):
        query_rows, leaf_key_rows, leaf_value_rows, cached_key_rows, cached_value_rows, parent_indices, visible_lengths = pieces
        head_list = [attend_single_head(query_rows[:, head_number], leaf_key_rows[:, head_number], leaf_value_rows[:, head_number], cached_key_rows[:, :, head_number], cached_value_rows[:, :, head_number], parent_indices, visible_lengths) for head_number in range(KEY_VALUE_HEADS)]
        return jnp.stack(head_list, axis=1)
    attended = lax.map(one_block, block_grid).reshape(LEAF_TOTAL, QUERY_HEADS * HEAD_WIDTH).astype(jnp.bfloat16)
    return jnp.dot(attended, dequantize(wo_quant, wo_scale), preferred_element_type=jnp.float32).astype(jnp.bfloat16)
```

```python
import functools
import math

import jax
import jax.numpy as jnp
from jax import lax
from jax.sharding import PartitionSpec as P

HEAD_WIDTH = 128
SCALE_BLOCK = 128


epsilon = 1e-06
rope_base = 1000000.0


def apply_rotary(values, length):
    width = values.shape[-1]
    half_width = width // 2
    freqs = rope_base ** (-(jnp.arange(half_width, dtype=jnp.float32) * 2.0 / width))
    angles = length.astype(jnp.float32)[:, None] * freqs[None, :]
    cosine = jnp.cos(angles)[:, None, :]
    sine = jnp.sin(angles)[:, None, :]
    first = values[..., :half_width]
    second = values[..., half_width:]
    return jnp.concatenate(
        [first * cosine - second * sine, second * cosine + first * sine], axis=-1
    )


def attend_single_head(
    query_vector, key_self, value_self, prefix_key_cache, prefix_value_cache, parent, length
):
    scale_factor = 1.0 / math.sqrt(query_vector.shape[-1])
    self_score = (
        jnp.sum(
            query_vector.astype(jnp.float32) * key_self.astype(jnp.float32)[:, None, :], axis=-1
        )
        * scale_factor
    )
    visible = (jnp.arange(prefix_key_cache.shape[1])[None, :] < length[:, None])[:, None, :]
    outcome = jnp.zeros(query_vector.shape, jnp.float32)
    for prefix_index in range(prefix_key_cache.shape[0]):
        scores = (
            jnp.einsum(
                "lge,ce->lgc",
                query_vector,
                prefix_key_cache[prefix_index],
                preferred_element_type=jnp.float32,
            )
            * scale_factor
        )
        highest = jnp.maximum(jnp.max(jnp.where(visible, scores, -jnp.inf), axis=-1), self_score)
        weights = jnp.where(visible, jnp.exp(scores - highest[..., None]), 0.0)
        self_weight = jnp.exp(self_score - highest)
        total = jnp.sum(weights, axis=-1) + self_weight
        self_rounded = lax.optimization_barrier(self_weight.astype(jnp.bfloat16)).astype(
            jnp.float32
        )
        mixed = jnp.einsum(
            "lgc,ce->lge",
            weights.astype(jnp.bfloat16),
            prefix_value_cache[prefix_index],
            preferred_element_type=jnp.float32,
        )
        mixed = mixed + self_rounded[..., None] * value_self.astype(jnp.float32)[:, None, :]
        outcome = jnp.where(
            (parent == prefix_index)[:, None, None], mixed / total[..., None], outcome
        )
    return outcome


def per_device(
    mesh_sizes,
    leaf_states,
    norm_gain,
    wq_quant,
    wq_scale,
    key_weight_quantized,
    key_weight_scale,
    value_weight_quantized,
    value_weight_scale,
    wo_quant,
    wo_scale,
    q_bias,
    key_bias,
    value_bias,
    prefix_key_cache,
    prefix_value_cache,
    parent_prefix_slot,
    prefix_length,
):
    n_job, n_actor = mesh_sizes
    swap = [(i, i ^ 1) for i in range(n_job)]
    side = lax.axis_index("job") % 2
    actor = lax.axis_index("actor")

    def trade(x):
        return lax.ppermute(x, "job", swap)

    states = leaf_states.astype(jnp.float32)
    normed = (
        states
        * lax.rsqrt(jnp.mean(states * states, axis=-1, keepdims=True) + epsilon)
        * norm_gain.astype(jnp.float32)
    ).astype(jnp.bfloat16)
    leaf_count = normed.shape[0]
    both_normed = jnp.concatenate([normed, trade(normed)], axis=0)
    both_length = jnp.concatenate([prefix_length, trade(prefix_length)], axis=0)

    def half_cols(x):
        width = x.shape[1] // 2
        return lax.dynamic_slice_in_dim(x, side * width, width, 1)

    row_count = wq_quant.shape[0]

    def expand_rows(quant, scale):
        mine = lax.dynamic_slice_in_dim(
            scale, actor * (row_count // SCALE_BLOCK), row_count // SCALE_BLOCK, 0
        ) if row_count % SCALE_BLOCK == 0 else None
        if mine is None:
            tall = jnp.repeat(scale, SCALE_BLOCK, axis=0)
            tall = lax.dynamic_slice_in_dim(tall, actor * row_count, row_count, 0)
        else:
            tall = jnp.repeat(mine, SCALE_BLOCK, axis=0)
        wide = jnp.repeat(half_cols(tall), SCALE_BLOCK, axis=1)
        return (half_cols(quant).astype(jnp.float32) * wide).astype(jnp.bfloat16)

    qkv_local = jnp.concatenate(
        [
            expand_rows(wq_quant, wq_scale),
            expand_rows(key_weight_quantized, key_weight_scale),
            expand_rows(value_weight_quantized, value_weight_scale),
        ],
        axis=1,
    )
    qkv_weight = lax.all_gather(qkv_local, "actor", axis=0, tiled=True)
    sums = jnp.dot(both_normed, qkv_weight, preferred_element_type=jnp.float32)

    def half_row(x):
        width = x.shape[0] // 2
        return lax.dynamic_slice_in_dim(x, side * width, width, 0)

    bias = jnp.concatenate([half_row(q_bias), half_row(key_bias), half_row(value_bias)])
    sums = sums + bias.astype(jnp.float32)
    v_width = value_bias.shape[0] // 2
    rot_width = sums.shape[1] - v_width
    rotated = apply_rotary(
        sums[:, :rot_width].reshape(2 * leaf_count, rot_width // HEAD_WIDTH, HEAD_WIDTH),
        both_length,
    ).reshape(2 * leaf_count, rot_width)
    done = jnp.concatenate([rotated, sums[:, rot_width:]], axis=1).astype(jnp.bfloat16)
    own = done[:leaf_count]
    other = trade(done[leaf_count:])
    q_width = q_bias.shape[0] // 2

    kv_half = v_width // HEAD_WIDTH
    query_group = q_bias.shape[0] // key_bias.shape[0]
    outs = []
    for which, block in ((side, own), (1 - side, other)):
        q = block[:, :q_width].reshape(leaf_count, kv_half, query_group, HEAD_WIDTH)
        k = block[:, q_width : q_width + v_width].reshape(leaf_count, kv_half, HEAD_WIDTH)
        v = block[:, q_width + v_width :].reshape(leaf_count, kv_half, HEAD_WIDTH)
        for head in range(kv_half):
            at = (which * kv_half + head) * HEAD_WIDTH
            outs.append(
                attend_single_head(
                    q[:, head],
                    k[:, head],
                    v[:, head],
                    lax.dynamic_slice_in_dim(prefix_key_cache, at, HEAD_WIDTH, 2),
                    lax.dynamic_slice_in_dim(prefix_value_cache, at, HEAD_WIDTH, 2),
                    parent_prefix_slot,
                    prefix_length,
                )
                .reshape(leaf_count, query_group * HEAD_WIDTH)
                .astype(jnp.bfloat16)
            )
    mine = jnp.concatenate(outs[:kv_half], axis=1)
    theirs = jnp.concatenate(outs[kv_half:], axis=1)
    attended = jnp.where(
        side == 0,
        jnp.concatenate([mine, theirs], axis=1),
        jnp.concatenate([theirs, mine], axis=1),
    )

    col_count = wo_quant.shape[1]
    spread_scale = jnp.repeat(wo_scale, SCALE_BLOCK, axis=1)
    own_scale = half_cols(lax.dynamic_slice_in_dim(spread_scale, actor * col_count, col_count, 1))
    wo_local = (
        half_cols(wo_quant).astype(jnp.float32) * jnp.repeat(own_scale, SCALE_BLOCK, axis=0)
    ).astype(jnp.bfloat16).T
    wo_all = lax.all_gather(wo_local, "actor", axis=0, tiled=True)
    both_attended = jnp.stack([attended, trade(attended)])
    group = lax.axis_index("tp")

    def project(rows):
        return lax.dot_general(
            rows, wo_all, (((1,), (1,)), ((), ())), preferred_element_type=jnp.float32
        )

    keep = project(lax.dynamic_index_in_dim(both_attended, group, 0, keepdims=False))
    give = project(lax.dynamic_index_in_dim(both_attended, 1 - group, 0, keepdims=False))
    got = lax.ppermute(give, "tp", [(0, 1), (1, 0)])
    total = (keep + got).astype(jnp.bfloat16)
    away = trade(total)
    local = jnp.where(group == 0, total, away)
    remote = lax.ppermute(local, "tp", [(0, 1), (1, 0)])
    mine_first = side == group
    low = jnp.where(mine_first, local, remote)
    high = jnp.where(mine_first, remote, local)
    pieces = []
    half = col_count // 2
    for a in range(n_actor):
        pieces += [low[:, a * half : (a + 1) * half], high[:, a * half : (a + 1) * half]]
    return jnp.concatenate(pieces, axis=1)


def solution(mesh):
    placed = (
        P(("job", "actor"), None),
        P(),
        P("actor", "tp"),
        P(None, "tp"),
        P("actor", "tp"),
        P(None, "tp"),
        P("actor", "tp"),
        P(None, "tp"),
        P("tp", "actor"),
        P("tp", None),
        P("tp"),
        P("tp"),
        P("tp"),
        P(("job", "actor"), None, "tp"),
        P(("job", "actor"), None, "tp"),
        P(("job", "actor")),
        P(("job", "actor")),
    )
    return jax.shard_map(
        functools.partial(per_device, (mesh.shape["job"], mesh.shape["actor"])),
        mesh=mesh,
        in_specs=placed,
        out_specs=P(("job", "actor"), None),
        check_vma=False,
    )
```

```python
import functools
import math

import jax
import jax.numpy as jnp
from jax import lax
from jax.experimental import pallas as pl
from jax.experimental.pallas import tpu as pltpu
from jax.sharding import PartitionSpec as P

HEAD_WIDTH = 128
SCALE_BLOCK = 128


epsilon = 1e-06
rope_base = 1000000.0


def apply_rotary(values, length):
    width = values.shape[-1]
    half_width = width // 2
    freqs = rope_base ** (-(jnp.arange(half_width, dtype=jnp.float32) * 2.0 / width))
    angles = length.astype(jnp.float32)[:, None] * freqs[None, :]
    cosine = jnp.cos(angles)[:, None, :]
    sine = jnp.sin(angles)[:, None, :]
    first = values[..., :half_width]
    second = values[..., half_width:]
    return jnp.concatenate(
        [first * cosine - second * sine, second * cosine + first * sine], axis=-1
    )


def attend_single_head(
    query_vector, key_self, value_self, prefix_key_cache, prefix_value_cache, parent, length
):
    scale_factor = 1.0 / math.sqrt(query_vector.shape[-1])
    self_score = (
        jnp.sum(
            query_vector.astype(jnp.float32) * key_self.astype(jnp.float32)[:, None, :], axis=-1
        )
        * scale_factor
    )
    visible = (jnp.arange(prefix_key_cache.shape[1])[None, :] < length[:, None])[:, None, :]
    outcome = jnp.zeros(query_vector.shape, jnp.float32)
    for prefix_index in range(prefix_key_cache.shape[0]):
        scores = (
            jnp.einsum(
                "lge,ce->lgc",
                query_vector,
                prefix_key_cache[prefix_index],
                preferred_element_type=jnp.float32,
            )
            * scale_factor
        )
        highest = jnp.maximum(jnp.max(jnp.where(visible, scores, -jnp.inf), axis=-1), self_score)
        weights = jnp.where(visible, jnp.exp(scores - highest[..., None]), 0.0)
        self_weight = jnp.exp(self_score - highest)
        total = jnp.sum(weights, axis=-1) + self_weight
        self_rounded = lax.optimization_barrier(self_weight.astype(jnp.bfloat16)).astype(
            jnp.float32
        )
        mixed = jnp.einsum(
            "lgc,ce->lge",
            weights.astype(jnp.bfloat16),
            prefix_value_cache[prefix_index],
            preferred_element_type=jnp.float32,
        )
        mixed = mixed + self_rounded[..., None] * value_self.astype(jnp.float32)[:, None, :]
        outcome = jnp.where(
            (parent == prefix_index)[:, None, None], mixed / total[..., None], outcome
        )
    return outcome


PIECE = 5
EARLY = 1


def spread_kernel(n_actor, rows_each, mine_ref, row_ref, all_ref, got_ref, home_sem, send_sem, recv_sem, row_sem):
    line = n_actor // 2
    actor = lax.axis_index("actor")
    job = lax.axis_index("job")
    at, y = actor // 2, actor % 2
    partner = job + 1 - 2 * (job % 2)
    pair = at * 2 + 1 - y
    has_up, has_down = at + 1 < line, at >= 1
    barrier = pltpu.get_barrier_semaphore()

    @pl.when(has_up)
    def _():
        pl.semaphore_signal(barrier, inc=1, device_id={"actor": actor + 2})

    @pl.when(has_down)
    def _():
        pl.semaphore_signal(barrier, inc=1, device_id={"actor": actor - 2})

    pl.semaphore_signal(barrier, inc=1, device_id={"actor": pair})
    pl.semaphore_signal(barrier, inc=1, device_id={"job": partner})
    pl.semaphore_wait(barrier, 2 + has_up.astype(jnp.int32) + has_down.astype(jnp.int32))

    def send(stream, source, piece, target, own=False):
        cut = pl.ds(piece * rows_each, rows_each)
        return pltpu.make_async_remote_copy(
            src_ref=mine_ref.at[cut] if own else all_ref.at[source, cut],
            dst_ref=all_ref.at[source, cut],
            send_sem=send_sem.at[stream, source, piece],
            recv_sem=recv_sem.at[source, piece],
            device_id={"actor": target},
        )

    def cross(source, piece, own=False):
        return send(0, source, piece, pair, own)

    def up(source, piece, own=False):
        return send(1, source, piece, actor + 2, own)

    def down(source, piece, own=False):
        return send(2, source, piece, actor - 2, own)

    def arrived(source, piece):
        cross(source, piece).wait_recv()

    late = list(range(PIECE - EARLY))
    early = list(range(PIECE - EARLY, PIECE))
    rows_copy = pltpu.make_async_remote_copy(
        src_ref=row_ref,
        dst_ref=got_ref,
        send_sem=row_sem.at[0],
        recv_sem=row_sem.at[1],
        device_id={"job": partner},
    )

    def both_ways(source, piece, own=False):
        @pl.when(has_up)
        def _():
            up(source, piece, own).start()

        @pl.when(has_down)
        def _():
            down(source, piece, own).start()

    for piece in early:
        cross(actor, piece, True).start()
    for piece in late:
        both_ways(actor, piece, True)
        cross(actor, piece, True).start()
    for piece in early:
        both_ways(actor, piece, True)
    rows_copy.start()
    home = pltpu.make_async_copy(mine_ref, all_ref.at[actor], home_sem)
    home.start()
    for piece in early:
        arrived(pair, piece)
        both_ways(pair, piece)
    for far in range(1, line):
        todo = [(y, p) for p in late] + [(y, p) for p in early] + [(1 - y, p) for p in early]
        for index, (which, piece) in enumerate(todo):
            below = (at - far) * 2 + which
            above = (at + far) * 2 + which

            @pl.when(at >= far)
            def _():
                arrived(below, piece)

                @pl.when(has_up)
                def _():
                    up(below, piece).start()

                if index < len(late):
                    cross(below, piece).start()

            @pl.when(at + far < line)
            def _():
                arrived(above, piece)

                @pl.when(has_down)
                def _():
                    down(above, piece).start()

                if index < len(late):
                    cross(above, piece).start()

    for spot in range(line):
        for piece in late:
            arrived(spot * 2 + 1 - y, piece)
    for spot in range(line):
        for piece in late:
            cross(spot * 2 + y, piece).wait_send()
    for piece in early:
        cross(actor, piece).wait_send()
    for spot in range(line):
        items = [(y, p) for p in range(PIECE)] + [(1 - y, p) for p in early]
        for which, piece in items:
            source = spot * 2 + which

            @pl.when(jnp.logical_and(has_up, at >= spot))
            def _():
                up(source, piece).wait_send()

            @pl.when(jnp.logical_and(has_down, at <= spot))
            def _():
                down(source, piece).wait_send()

    rows_copy.wait()
    home.wait()


def spread(shard, rows, n_actor):
    height = shard.shape[0]
    return pl.pallas_call(
        functools.partial(spread_kernel, n_actor, height // PIECE),
        out_shape=(
            jax.ShapeDtypeStruct((n_actor,) + shard.shape, shard.dtype),
            jax.ShapeDtypeStruct(rows.shape, rows.dtype),
        ),
        in_specs=[pl.BlockSpec(memory_space=pl.ANY)] * 2,
        out_specs=(pl.BlockSpec(memory_space=pl.ANY),) * 2,
        scratch_shapes=[
            pltpu.SemaphoreType.DMA,
            pltpu.SemaphoreType.DMA((3, n_actor, PIECE)),
            pltpu.SemaphoreType.DMA((n_actor, PIECE)),
            pltpu.SemaphoreType.DMA((2,)),
        ],
        compiler_params=pltpu.CompilerParams(collective_id=0, has_side_effects=True),
        cost_estimate=pl.CostEstimate(
            flops=0, bytes_accessed=300_000_000, transcendentals=0
        ),
    )(shard, rows)


def per_device(
    mesh_sizes,
    leaf_states,
    norm_gain,
    wq_quant,
    wq_scale,
    key_weight_quantized,
    key_weight_scale,
    value_weight_quantized,
    value_weight_scale,
    wo_quant,
    wo_scale,
    q_bias,
    key_bias,
    value_bias,
    prefix_key_cache,
    prefix_value_cache,
    parent_prefix_slot,
    prefix_length,
):
    n_job, n_actor = mesh_sizes
    swap = [(i, i ^ 1) for i in range(n_job)]
    side = lax.axis_index("job") % 2
    actor = lax.axis_index("actor")

    def trade(x):
        return lax.ppermute(x, "job", swap)

    states = leaf_states.astype(jnp.float32)
    normed = (
        states
        * lax.rsqrt(jnp.mean(states * states, axis=-1, keepdims=True) + epsilon)
        * norm_gain.astype(jnp.float32)
    ).astype(jnp.bfloat16)
    leaf_count = normed.shape[0]
    both_length = jnp.concatenate([prefix_length, trade(prefix_length)], axis=0)

    def half_cols(x):
        width = x.shape[1] // 2
        return lax.dynamic_slice_in_dim(x, side * width, width, 1)

    row_count = wq_quant.shape[0]

    def expand_rows(quant, scale):
        mine = lax.dynamic_slice_in_dim(
            scale, actor * (row_count // SCALE_BLOCK), row_count // SCALE_BLOCK, 0
        ) if row_count % SCALE_BLOCK == 0 else None
        if mine is None:
            tall = jnp.repeat(scale, SCALE_BLOCK, axis=0)
            tall = lax.dynamic_slice_in_dim(tall, actor * row_count, row_count, 0)
        else:
            tall = jnp.repeat(mine, SCALE_BLOCK, axis=0)
        wide = jnp.repeat(half_cols(tall), SCALE_BLOCK, axis=1)
        return (half_cols(quant).astype(jnp.float32) * wide).astype(jnp.bfloat16)

    qkv_local = jnp.concatenate(
        [
            expand_rows(wq_quant, wq_scale),
            expand_rows(key_weight_quantized, key_weight_scale),
            expand_rows(value_weight_quantized, value_weight_scale),
        ],
        axis=1,
    )
    col_count = wo_quant.shape[1]
    spread_scale = jnp.repeat(wo_scale, SCALE_BLOCK, axis=1)
    own_scale = half_cols(lax.dynamic_slice_in_dim(spread_scale, actor * col_count, col_count, 1))
    wo_local = (
        half_cols(wo_quant).astype(jnp.float32) * jnp.repeat(own_scale, SCALE_BLOCK, axis=0)
    ).astype(jnp.bfloat16).T
    qkv_weight, other_normed = spread(qkv_local, normed, n_actor)
    qkv_weight = qkv_weight.reshape(-1, qkv_local.shape[1])
    wo_local, qkv_weight = lax.optimization_barrier((wo_local, qkv_weight))
    both_normed = jnp.concatenate([normed, other_normed], axis=0)
    sums = jnp.dot(both_normed, qkv_weight, preferred_element_type=jnp.float32)

    def half_row(x):
        width = x.shape[0] // 2
        return lax.dynamic_slice_in_dim(x, side * width, width, 0)

    bias = jnp.concatenate([half_row(q_bias), half_row(key_bias), half_row(value_bias)])
    sums = sums + bias.astype(jnp.float32)
    v_width = value_bias.shape[0] // 2
    rot_width = sums.shape[1] - v_width
    rotated = apply_rotary(
        sums[:, :rot_width].reshape(2 * leaf_count, rot_width // HEAD_WIDTH, HEAD_WIDTH),
        both_length,
    ).reshape(2 * leaf_count, rot_width)
    done = jnp.concatenate([rotated, sums[:, rot_width:]], axis=1).astype(jnp.bfloat16)
    own = done[:leaf_count]
    other = trade(done[leaf_count:])
    q_width = q_bias.shape[0] // 2

    kv_half = v_width // HEAD_WIDTH
    query_group = q_bias.shape[0] // key_bias.shape[0]
    outs = []
    for which, block in ((side, own), (1 - side, other)):
        q = block[:, :q_width].reshape(leaf_count, kv_half, query_group, HEAD_WIDTH)
        k = block[:, q_width : q_width + v_width].reshape(leaf_count, kv_half, HEAD_WIDTH)
        v = block[:, q_width + v_width :].reshape(leaf_count, kv_half, HEAD_WIDTH)
        for head in range(kv_half):
            at = (which * kv_half + head) * HEAD_WIDTH
            outs.append(
                attend_single_head(
                    q[:, head],
                    k[:, head],
                    v[:, head],
                    lax.dynamic_slice_in_dim(prefix_key_cache, at, HEAD_WIDTH, 2),
                    lax.dynamic_slice_in_dim(prefix_value_cache, at, HEAD_WIDTH, 2),
                    parent_prefix_slot,
                    prefix_length,
                )
                .reshape(leaf_count, query_group * HEAD_WIDTH)
                .astype(jnp.bfloat16)
            )
    mine = jnp.concatenate(outs[:kv_half], axis=1)
    theirs = jnp.concatenate(outs[kv_half:], axis=1)
    attended = jnp.where(
        side == 0,
        jnp.concatenate([mine, theirs], axis=1),
        jnp.concatenate([theirs, mine], axis=1),
    )

    wo_all = lax.all_gather(wo_local, "actor", axis=0, tiled=True)
    group = lax.axis_index("tp")
    cores = [(0, 1), (1, 0)]

    def project(rows):
        part = lax.dot_general(
            rows, wo_all, (((1,), (1,)), ((), ())), preferred_element_type=jnp.float32
        )
        width = part.shape[1] // 2
        first, second = part[:, :width], part[:, width:]
        give = jnp.where(group == 0, second, first)
        keep = jnp.where(group == 0, first, second)
        return (keep + lax.ppermute(give, "tp", cores)).astype(jnp.bfloat16), give

    def join(x):
        y = lax.ppermute(x, "tp", cores)
        return jnp.where(
            group == 0,
            jnp.concatenate([x, y], axis=1),
            jnp.concatenate([y, x], axis=1),
        )

    away, marker = project(trade(attended))
    attended, away, _ = lax.optimization_barrier((attended, away, marker))
    away = trade(away)
    local = join(project(attended)[0])
    remote = join(away)
    low = jnp.where(side == 0, local, remote)
    high = jnp.where(side == 0, remote, local)
    pieces = []
    half = col_count // 2
    for a in range(n_actor):
        pieces += [low[:, a * half : (a + 1) * half], high[:, a * half : (a + 1) * half]]
    return jnp.concatenate(pieces, axis=1)


def solution(mesh):
    placed = (
        P(("job", "actor"), None),
        P(),
        P("actor", "tp"),
        P(None, "tp"),
        P("actor", "tp"),
        P(None, "tp"),
        P("actor", "tp"),
        P(None, "tp"),
        P("tp", "actor"),
        P("tp", None),
        P("tp"),
        P("tp"),
        P("tp"),
        P(("job", "actor"), None, "tp"),
        P(("job", "actor"), None, "tp"),
        P(("job", "actor")),
        P(("job", "actor")),
    )
    return jax.shard_map(
        functools.partial(per_device, (mesh.shape["job"], mesh.shape["actor"])),
        mesh=mesh,
        in_specs=placed,
        out_specs=P(("job", "actor"), None),
        check_vma=False,
    )
```

```python
import functools
import math

import jax
import jax.numpy as jnp
from jax import lax
from jax.experimental import pallas as pl
from jax.experimental.pallas import tpu as pltpu
from jax.sharding import PartitionSpec as P

HEAD_WIDTH = 128
SCALE_BLOCK = 128


epsilon = 1e-06
rope_base = 1000000.0


def apply_rotary(values, length):
    width = values.shape[-1]
    half_width = width // 2
    freqs = rope_base ** (-(jnp.arange(half_width, dtype=jnp.float32) * 2.0 / width))
    angles = length.astype(jnp.float32)[:, None] * freqs[None, :]
    cosine = jnp.cos(angles)[:, None, :]
    sine = jnp.sin(angles)[:, None, :]
    first = values[..., :half_width]
    second = values[..., half_width:]
    return jnp.concatenate(
        [first * cosine - second * sine, second * cosine + first * sine], axis=-1
    )


def attend_single_head(
    query_vector, key_self, value_self, prefix_key_cache, prefix_value_cache, parent, length
):
    scale_factor = 1.0 / math.sqrt(query_vector.shape[-1])
    self_score = (
        jnp.sum(
            query_vector.astype(jnp.float32) * key_self.astype(jnp.float32)[:, None, :], axis=-1
        )
        * scale_factor
    )
    visible = (jnp.arange(prefix_key_cache.shape[1])[None, :] < length[:, None])[:, None, :]
    outcome = jnp.zeros(query_vector.shape, jnp.float32)
    for prefix_index in range(prefix_key_cache.shape[0]):
        scores = (
            jnp.einsum(
                "lge,ce->lgc",
                query_vector,
                prefix_key_cache[prefix_index],
                preferred_element_type=jnp.float32,
            )
            * scale_factor
        )
        highest = jnp.maximum(jnp.max(jnp.where(visible, scores, -jnp.inf), axis=-1), self_score)
        weights = jnp.where(visible, jnp.exp(scores - highest[..., None]), 0.0)
        self_weight = jnp.exp(self_score - highest)
        total = jnp.sum(weights, axis=-1) + self_weight
        self_rounded = lax.optimization_barrier(self_weight.astype(jnp.bfloat16)).astype(
            jnp.float32
        )
        mixed = jnp.einsum(
            "lgc,ce->lge",
            weights.astype(jnp.bfloat16),
            prefix_value_cache[prefix_index],
            preferred_element_type=jnp.float32,
        )
        mixed = mixed + self_rounded[..., None] * value_self.astype(jnp.float32)[:, None, :]
        outcome = jnp.where(
            (parent == prefix_index)[:, None, None], mixed / total[..., None], outcome
        )
    return outcome


PIECE = 5
EARLY = 1


def spread_kernel(
    n_actor,
    rows_each,
    mine_ref,
    row_ref,
    gain_ref,
    sums_ref,
    all_ref,
    raw_ref,
    x_ref,
    home_sem,
    send_sem,
    recv_sem,
    row_sem,
):
    line = n_actor // 2
    actor = lax.axis_index("actor")
    job = lax.axis_index("job")
    at, y = actor // 2, actor % 2
    partner = job + 1 - 2 * (job % 2)
    pair = at * 2 + 1 - y
    has_up, has_down = at + 1 < line, at >= 1
    count = row_ref.shape[0]
    depth = mine_ref.shape[0]
    barrier = pltpu.get_barrier_semaphore()

    @pl.when(has_up)
    def _():
        pl.semaphore_signal(barrier, inc=1, device_id={"actor": actor + 2})

    @pl.when(has_down)
    def _():
        pl.semaphore_signal(barrier, inc=1, device_id={"actor": actor - 2})

    pl.semaphore_signal(barrier, inc=1, device_id={"actor": pair})
    pl.semaphore_signal(barrier, inc=1, device_id={"job": partner})
    pl.semaphore_wait(barrier, 2 + has_up.astype(jnp.int32) + has_down.astype(jnp.int32))

    def send(stream, source, piece, target, own=False):
        cut = pl.ds(piece * rows_each, rows_each)
        return pltpu.make_async_remote_copy(
            src_ref=mine_ref.at[cut] if own else all_ref.at[source, cut],
            dst_ref=all_ref.at[source, cut],
            send_sem=send_sem.at[stream, source, piece],
            recv_sem=recv_sem.at[source, piece],
            device_id={"actor": target},
        )

    def cross(source, piece, own=False):
        return send(0, source, piece, pair, own)

    def up(source, piece, own=False):
        return send(1, source, piece, actor + 2, own)

    def down(source, piece, own=False):
        return send(2, source, piece, actor - 2, own)

    def arrived(source, piece):
        cross(source, piece).wait_recv()

    late = list(range(PIECE - EARLY))
    early = list(range(PIECE - EARLY, PIECE))
    rows_copy = pltpu.make_async_remote_copy(
        src_ref=row_ref,
        dst_ref=raw_ref.at[pl.ds(count, count)],
        send_sem=row_sem.at[0],
        recv_sem=row_sem.at[1],
        device_id={"job": partner},
    )

    def both_ways(source, piece, own=False):
        @pl.when(has_up)
        def _():
            up(source, piece, own).start()

        @pl.when(has_down)
        def _():
            down(source, piece, own).start()

    for piece in early:
        cross(actor, piece, True).start()
    for piece in late:
        both_ways(actor, piece, True)
        cross(actor, piece, True).start()
    for piece in early:
        both_ways(actor, piece, True)
    rows_copy.start()
    home = pltpu.make_async_copy(mine_ref, all_ref.at[actor], home_sem.at[0])
    home.start()
    own_rows = pltpu.make_async_copy(row_ref, raw_ref.at[pl.ds(0, count)], home_sem.at[1])
    own_rows.start()

    def normalize(first):
        def block(i, carry):
            cut = pl.ds(pl.multiple_of(first + i * 16, 16), 16)
            rows = raw_ref[cut, :].astype(jnp.float32)
            rows = rows * lax.rsqrt(jnp.mean(rows * rows, axis=-1, keepdims=True) + epsilon)
            rows = (rows * gain_ref[...].astype(jnp.float32)).astype(jnp.bfloat16)
            for source in range(n_actor):
                x_ref[source, cut, :] = rows[:, source * depth : (source + 1) * depth]
            return carry

        lax.fori_loop(0, count // 16, block, 0)

    def add(source):
        sums_ref[...] += jnp.dot(
            x_ref[source], all_ref[source], preferred_element_type=jnp.float32
        )

    sums_ref[...] = jnp.zeros_like(sums_ref)
    own_rows.wait()
    normalize(0)
    for piece in early:
        arrived(pair, piece)
        both_ways(pair, piece)
    turn = jnp.where(at * 2 < line, 1, line - 1)

    def spot_of(k):
        return lax.rem(at + k * turn, line)

    for far in range(1, line):
        if far == line - 1:
            rows_copy.wait()
            normalize(count)
            home.wait()
            add(actor)
        todo = [(y, p) for p in late] + [(y, p) for p in early] + [(1 - y, p) for p in early]
        for index, (which, piece) in enumerate(todo):
            below = (at - far) * 2 + which
            above = (at + far) * 2 + which

            @pl.when(at >= far)
            def _():
                arrived(below, piece)

                @pl.when(has_up)
                def _():
                    up(below, piece).start()

                if index < len(late):
                    cross(below, piece).start()

            @pl.when(at + far < line)
            def _():
                arrived(above, piece)

                @pl.when(has_down)
                def _():
                    down(above, piece).start()

                if index < len(late):
                    cross(above, piece).start()

    def add_held(k, carry):
        add(spot_of(k) * 2 + y)
        return carry

    lax.fori_loop(1, line, add_held, 0)

    def add_crossed(k, carry):
        source = spot_of(k) * 2 + 1 - y
        for piece in late:
            arrived(source, piece)
        add(source)
        return carry

    lax.fori_loop(0, line, add_crossed, 0)
    for spot in range(line):
        for piece in late:
            cross(spot * 2 + y, piece).wait_send()
    for piece in early:
        cross(actor, piece).wait_send()
    for spot in range(line):
        items = [(y, p) for p in range(PIECE)] + [(1 - y, p) for p in early]
        for which, piece in items:
            source = spot * 2 + which

            @pl.when(jnp.logical_and(has_up, at >= spot))
            def _():
                up(source, piece).wait_send()

            @pl.when(jnp.logical_and(has_down, at <= spot))
            def _():
                down(source, piece).wait_send()


def spread(shard, rows, gain, n_actor):
    height, width = shard.shape
    return pl.pallas_call(
        functools.partial(spread_kernel, n_actor, height // PIECE),
        out_shape=jax.ShapeDtypeStruct((2 * rows.shape[0], width), jnp.float32),
        in_specs=[
            pl.BlockSpec(memory_space=pl.ANY),
            pl.BlockSpec(memory_space=pl.ANY),
            pl.BlockSpec(memory_space=pltpu.VMEM),
        ],
        out_specs=pl.BlockSpec(memory_space=pltpu.VMEM),
        scratch_shapes=[
            pltpu.VMEM((n_actor,) + shard.shape, shard.dtype),
            pltpu.VMEM((2 * rows.shape[0], rows.shape[1]), rows.dtype),
            pltpu.VMEM((n_actor, 2 * rows.shape[0], height), rows.dtype),
            pltpu.SemaphoreType.DMA((2,)),
            pltpu.SemaphoreType.DMA((3, n_actor, PIECE)),
            pltpu.SemaphoreType.DMA((n_actor, PIECE)),
            pltpu.SemaphoreType.DMA((2,)),
        ],
        compiler_params=pltpu.CompilerParams(
            collective_id=0, has_side_effects=True, vmem_limit_bytes=48 * 1024 * 1024
        ),
        cost_estimate=pl.CostEstimate(
            flops=0, bytes_accessed=300_000_000, transcendentals=0
        ),
    )(shard, rows, gain)


def per_device(
    mesh_sizes,
    leaf_states,
    norm_gain,
    wq_quant,
    wq_scale,
    key_weight_quantized,
    key_weight_scale,
    value_weight_quantized,
    value_weight_scale,
    wo_quant,
    wo_scale,
    q_bias,
    key_bias,
    value_bias,
    prefix_key_cache,
    prefix_value_cache,
    parent_prefix_slot,
    prefix_length,
):
    n_job, n_actor = mesh_sizes
    swap = [(i, i ^ 1) for i in range(n_job)]
    side = lax.axis_index("job") % 2
    actor = lax.axis_index("actor")

    def trade(x):
        return lax.ppermute(x, "job", swap)

    leaf_count = leaf_states.shape[0]

    def half_cols(x):
        width = x.shape[1] // 2
        return lax.dynamic_slice_in_dim(x, side * width, width, 1)

    row_count = wq_quant.shape[0]

    def expand_rows(quant, scale):
        mine = lax.dynamic_slice_in_dim(
            scale, actor * (row_count // SCALE_BLOCK), row_count // SCALE_BLOCK, 0
        ) if row_count % SCALE_BLOCK == 0 else None
        if mine is None:
            tall = jnp.repeat(scale, SCALE_BLOCK, axis=0)
            tall = lax.dynamic_slice_in_dim(tall, actor * row_count, row_count, 0)
        else:
            tall = jnp.repeat(mine, SCALE_BLOCK, axis=0)
        wide = jnp.repeat(half_cols(tall), SCALE_BLOCK, axis=1)
        return (half_cols(quant).astype(jnp.float32) * wide).astype(jnp.bfloat16)

    qkv_local = jnp.concatenate(
        [
            expand_rows(wq_quant, wq_scale),
            expand_rows(key_weight_quantized, key_weight_scale),
            expand_rows(value_weight_quantized, value_weight_scale),
        ],
        axis=1,
    )
    col_count = wo_quant.shape[1]
    spread_scale = jnp.repeat(wo_scale, SCALE_BLOCK, axis=1)
    own_scale = half_cols(lax.dynamic_slice_in_dim(spread_scale, actor * col_count, col_count, 1))
    wo_local = (
        half_cols(wo_quant).astype(jnp.float32) * jnp.repeat(own_scale, SCALE_BLOCK, axis=0)
    ).astype(jnp.bfloat16).T
    sums = spread(qkv_local, leaf_states, norm_gain[None, :], n_actor)
    wo_local, sums, prefix_length = lax.optimization_barrier((wo_local, sums, prefix_length))
    both_length = jnp.concatenate([prefix_length, trade(prefix_length)], axis=0)

    def half_row(x):
        width = x.shape[0] // 2
        return lax.dynamic_slice_in_dim(x, side * width, width, 0)

    bias = jnp.concatenate([half_row(q_bias), half_row(key_bias), half_row(value_bias)])
    sums = sums + bias.astype(jnp.float32)
    v_width = value_bias.shape[0] // 2
    rot_width = sums.shape[1] - v_width
    rotated = apply_rotary(
        sums[:, :rot_width].reshape(2 * leaf_count, rot_width // HEAD_WIDTH, HEAD_WIDTH),
        both_length,
    ).reshape(2 * leaf_count, rot_width)
    done = jnp.concatenate([rotated, sums[:, rot_width:]], axis=1).astype(jnp.bfloat16)
    own = done[:leaf_count]
    other = trade(done[leaf_count:])
    q_width = q_bias.shape[0] // 2

    kv_half = v_width // HEAD_WIDTH
    query_group = q_bias.shape[0] // key_bias.shape[0]
    outs = []
    for which, block in ((side, own), (1 - side, other)):
        q = block[:, :q_width].reshape(leaf_count, kv_half, query_group, HEAD_WIDTH)
        k = block[:, q_width : q_width + v_width].reshape(leaf_count, kv_half, HEAD_WIDTH)
        v = block[:, q_width + v_width :].reshape(leaf_count, kv_half, HEAD_WIDTH)
        for head in range(kv_half):
            at = (which * kv_half + head) * HEAD_WIDTH
            outs.append(
                attend_single_head(
                    q[:, head],
                    k[:, head],
                    v[:, head],
                    lax.dynamic_slice_in_dim(prefix_key_cache, at, HEAD_WIDTH, 2),
                    lax.dynamic_slice_in_dim(prefix_value_cache, at, HEAD_WIDTH, 2),
                    parent_prefix_slot,
                    prefix_length,
                )
                .reshape(leaf_count, query_group * HEAD_WIDTH)
                .astype(jnp.bfloat16)
            )
    mine = jnp.concatenate(outs[:kv_half], axis=1)
    theirs = jnp.concatenate(outs[kv_half:], axis=1)
    attended = jnp.where(
        side == 0,
        jnp.concatenate([mine, theirs], axis=1),
        jnp.concatenate([theirs, mine], axis=1),
    )

    wo_all = lax.all_gather(wo_local, "actor", axis=0, tiled=True)
    group = lax.axis_index("tp")
    cores = [(0, 1), (1, 0)]

    def project(rows):
        part = lax.dot_general(
            rows, wo_all, (((1,), (1,)), ((), ())), preferred_element_type=jnp.float32
        )
        width = part.shape[1] // 2
        first, second = part[:, :width], part[:, width:]
        give = jnp.where(group == 0, second, first)
        keep = jnp.where(group == 0, first, second)
        return (keep + lax.ppermute(give, "tp", cores)).astype(jnp.bfloat16), give

    def join(x):
        y = lax.ppermute(x, "tp", cores)
        return jnp.where(
            group == 0,
            jnp.concatenate([x, y], axis=1),
            jnp.concatenate([y, x], axis=1),
        )

    away, marker = project(trade(attended))
    attended, away, _ = lax.optimization_barrier((attended, away, marker))
    away = trade(away)
    local = join(project(attended)[0])
    remote = join(away)
    low = jnp.where(side == 0, local, remote)
    high = jnp.where(side == 0, remote, local)
    pieces = []
    half = col_count // 2
    for a in range(n_actor):
        pieces += [low[:, a * half : (a + 1) * half], high[:, a * half : (a + 1) * half]]
    return jnp.concatenate(pieces, axis=1)


def solution(mesh):
    placed = (
        P(("job", "actor"), None),
        P(),
        P("actor", "tp"),
        P(None, "tp"),
        P("actor", "tp"),
        P(None, "tp"),
        P("actor", "tp"),
        P(None, "tp"),
        P("tp", "actor"),
        P("tp", None),
        P("tp"),
        P("tp"),
        P("tp"),
        P(("job", "actor"), None, "tp"),
        P(("job", "actor"), None, "tp"),
        P(("job", "actor")),
        P(("job", "actor")),
    )
    return jax.shard_map(
        functools.partial(per_device, (mesh.shape["job"], mesh.shape["actor"])),
        mesh=mesh,
        in_specs=placed,
        out_specs=P(("job", "actor"), None),
        check_vma=False,
    )
```
